512 devices in a mesh: section: 32 (over z_lo, y, core), rep: 16 (over z_hi, x).
Axes of the slice: x: 4, y: 8, z: 8 (z_hi: 4, z_lo: 2; z = z_hi * 2 + z_lo), core: 2. Of those that a mesh axis runs over, the one named last changes fastest.
Arguments:
- tokens: bfloat16 [32, 16, 256, 1024], P('section', 'rep'), may hold values from -6 to 6
- assign: int32 [32, 16, 256, 1], P('section', 'rep'), may hold values from 0 to 31; in each aligned block of 256 rows (0 to 255, 256 to 511, ..., all dimensions but the last counted through in order) at most 12 rows name the same one
- route_mask: int32 [32], replicated, may hold values from 1 to 15
- match_mask: int32 [32], replicated, may hold values from 1 to 15
- gate_weight: bfloat16 [32, 16, 1024, 256], P('section', 'rep'), may hold values from -0.1875 to 0.1875
- up_weight: bfloat16 [32, 16, 1024, 256], P('section', 'rep'), may hold values from -0.1875 to 0.1875
- down_weight: bfloat16 [32, 16, 256, 1024], P('section', 'rep'), may hold values from -0.375 to 0.375
- slow_down: bfloat16 [32, 16, 256, 1024], P('section', 'rep'), may hold values from -4 to 4
- momentum: bfloat16 [32, 16, 256, 1024], P('section', 'rep'), may hold values from -4 to 4
- slot_cot: bfloat16 [32, 16, 32, 12, 1024], P('section', 'rep'), may hold values from -6 to 6
Outputs:
- input_grad: bfloat16 [32, 16, 256, 1024], P('section', 'rep')
- new_slow: bfloat16 [32, 16, 256, 1024], P('section', 'rep')
The draws below stay inside these ranges and needn't reach their ends.
Inputs may be any that keep to these rules, and one draw needn't show every extreme that they name: `assign`: no expert is named by more than 12 rows of one device, and in every draw some device has 12 rows for one expert. Rows that replica r of any section sends to expert e are processed by replica r XOR route_mask[e] of that expert. Replica r of section s is matched with replica r XOR match_mask[s].
All inputs are finite; a program needn't handle non-finite values.
Results may differ from the reference program's by a relative error of at most 0.012.
Values may be sent and summed in bfloat16 or wider, within the bound.
A program may use at most 64 MiB of HBM per device.

```python
import math
import jax
import jax.numpy as jnp
import numpy as np
from jax import lax

D = 1024
FF = 256
TOK_DEV = 256
CAP = 12
N_SECTION = 32
N_REP = 16


def plant(drawn, own_key, low, top_value):
    index_at = [jax.random.randint(jax.random.fold_in(own_key, axis), (), 0, length) for axis, length in enumerate(drawn.shape)]
    main_axis = drawn.shape.index(max(drawn.shape))
    beside = index_at[:main_axis] + [(index_at[main_axis] + 1) % drawn.shape[main_axis]] + index_at[main_axis + 1:]
    return drawn.at[tuple(index_at)].set(low).at[tuple(beside)].set(top_value)


def steps_of(stream_key, dims, shards, smallest, largest):
    factor_of, own = 1.0, jax.random.fold_in(stream_key, 6)
    for dim, parts in shards:
        draws = jnp.exp(jax.random.uniform(jax.random.fold_in(own, dim), (parts,), jnp.float32, smallest / len(shards), largest / len(shards)))
        factor_of = factor_of * jnp.repeat(draws, dims[dim] // parts).reshape([-1 if axis == dim else 1 for axis in range(len(dims))])
    return factor_of


def routed_block(own_key, own, number, rows, amount, top, bound, lean):
    order = jax.random.permutation(own_key, amount)
    heavy_load, usual = portions_of(amount, rows * top, bound, lean, True), portions_of(amount, rows * top, bound, lean, False)
    places = jnp.arange(amount)

    def named(sizes, rotation):
        used = int((sizes > 0).sum())
        fixed = max(1, used // 4)
        moved = fixed + (places - fixed + rotation * (used - fixed)) % max(1, amount - fixed)
        return jnp.zeros((amount,), jnp.int32).at[order[jnp.where(places < fixed, places, moved)]].set(jnp.asarray(sizes, jnp.int32))

    sizes = jnp.where(number % 4 == 0, named(heavy_load, number // 4), named(usual, number - number // 4 - 1))
    mixed = jax.random.permutation(jax.random.fold_in(own, 3), amount)
    giver, receiver = mixed[0:amount // 2 * 2:2], mixed[1:amount // 2 * 2:2]
    room = jnp.minimum(sizes[giver] - 1, bound - sizes[receiver]) // 2
    room = jnp.where((giver == order[0]) | (receiver == order[0]) | (sizes[receiver] == 0), 0, jnp.maximum(room, 0))
    moved = jax.random.randint(jax.random.fold_in(own, 4), (amount // 2,), 0, 1 << 20) % (room + 1)
    sizes = sizes.at[giver].add(-moved).at[receiver].add(moved)
    items = jnp.searchsorted(jnp.cumsum(sizes), jnp.arange(rows * top), side="right").astype(jnp.int32)
    table = items.reshape(top, rows).T
    table = table[jax.random.permutation(jax.random.fold_in(own, 1), rows)]
    rotation = jax.random.randint(jax.random.fold_in(own, 2), (rows, 1), 0, top)
    return jnp.take_along_axis(table, (jnp.arange(top)[None, :] + rotation) % top, axis=1)


def portions_of(count, total, reach, lean, full):
    portions = [(1 << 20) // math.isqrt(grade ** lean) + 1 for grade in range(1, count + 1)]
    largest = reach if full else min(reach, max(-(-total // count), total * portions[0] // sum(portions)))
    least = 1 if total - largest >= count - 1 else 0
    given, spare = [largest] + [least] * (count - 1), total - largest - least * (count - 1)
    while spare > 0:
        movable = [i for i in range(1, count) if given[i] < largest] or [i for i in range(1, count) if given[i] < reach]
        mass, budget = sum([portions[i] for i in movable]), spare
        for i in movable:
            extra = min(reach - given[i], max(1, budget * portions[i] // mass), spare)
            given[i] = given[i] + extra
            spare = spare - extra
    return np.array(given)


def bell_draw(own_key, dims, width, reach, split=(), kind=jnp.bfloat16):
    factor_of = steps_of(own_key, dims, split, -0.22, 0.18) if split else 1.0
    array = jax.random.normal(own_key, dims, jnp.float32) * width * factor_of
    return jnp.minimum(jnp.maximum(array, -reach), reach).astype(kind)


def setup_inputs(seed: int = 0) -> dict:
    arg_keys = jax.random.split(jax.random.key(seed), 11)
    tokens = bell_draw(arg_keys[0], (N_SECTION, N_REP, TOK_DEV, D), 1.0, 6.0, ((0, 32), (1, 16)))
    assign_keys = jax.random.split(jax.random.fold_in(arg_keys[1], 1), N_SECTION * N_REP * TOK_DEV // TOK_DEV)
    assign_turns = jax.random.permutation(jax.random.fold_in(arg_keys[1], 3), N_SECTION * N_REP * TOK_DEV // TOK_DEV)
    assign = jax.vmap(lambda own, number: routed_block(jax.random.fold_in(arg_keys[1], 2), own, number, TOK_DEV, N_SECTION, 1, CAP, 2))(assign_keys, assign_turns).reshape((N_SECTION, N_REP, TOK_DEV, 1))
    route_mask = plant(jax.random.randint(arg_keys[2], (N_SECTION,), 1, N_REP), jax.random.fold_in(arg_keys[2], 1), 1, N_REP - 1).astype(jnp.int32)
    match_mask = plant(jax.random.randint(arg_keys[3], (N_SECTION,), 1, N_REP), jax.random.fold_in(arg_keys[3], 1), 1, N_REP - 1).astype(jnp.int32)
    gate_weight = bell_draw(arg_keys[4], (N_SECTION, N_REP, D, FF), D ** -0.5, 0.1875, ((0, 32), (1, 16)))
    up_weight = bell_draw(arg_keys[5], (N_SECTION, N_REP, D, FF), D ** -0.5, 0.1875, ((0, 32), (1, 16)))
    down_weight = bell_draw(arg_keys[6], (N_SECTION, N_REP, FF, D), FF ** -0.5, 0.375, ((0, 32), (1, 16)))
    slow_down = bell_draw(arg_keys[7], (N_SECTION, N_REP, FF, D), 0.5, 4.0, ((0, 32), (1, 16)))
    momentum = bell_draw(arg_keys[8], (N_SECTION, N_REP, FF, D), 0.5, 4.0, ((0, 32), (1, 16)))
    slot_cot = bell_draw(arg_keys[9], (N_SECTION, N_REP, N_SECTION, CAP, D), 1.0, 6.0, ((0, 32), (1, 16)))
    return {"tokens": tokens, "assign": assign, "route_mask": route_mask, "match_mask": match_mask, "gate_weight": gate_weight, "up_weight": up_weight, "down_weight": down_weight, "slow_down": slow_down, "momentum": momentum, "slot_cot": slot_cot}


inner_rate = 0.05
pull_rate = 0.25
moment_rate = 0.9
outer_rate = 0.7


def slot_table(expert_ids, sections, capacity):
    expert_hot = (expert_ids[:, None] == jnp.arange(sections, dtype=jnp.int32)[None, :]).astype(jnp.int32)
    position = jnp.sum((jnp.cumsum(expert_hot, axis=0) - 1) * expert_hot, axis=1)
    slot_index = expert_ids * capacity + position
    return (slot_index[:, None] == jnp.arange(sections * capacity, dtype=jnp.int32)[None, :]).astype(jnp.bfloat16)


def expert_pass(rows, cotangent, gate_mat, up_mat, down_mat):
    contract = (((1,), (1,)), ((), ()))
    gate_act = jnp.dot(rows, gate_mat, preferred_element_type=jnp.float32)
    up_act = jnp.dot(rows, up_mat, preferred_element_type=jnp.float32)
    sigmoid_gate = jax.nn.sigmoid(gate_act)
    hidden = (gate_act * sigmoid_gate * up_act).astype(jnp.bfloat16)
    hidden_grad = lax.dot_general(cotangent, down_mat, contract, preferred_element_type=jnp.float32)
    gate_grad = (hidden_grad * up_act * sigmoid_gate * (1.0 + gate_act * (1.0 - sigmoid_gate))).astype(jnp.bfloat16)
    up_grad = (hidden_grad * gate_act * sigmoid_gate).astype(jnp.bfloat16)
    slot_grad = (lax.dot_general(gate_grad, gate_mat, contract, preferred_element_type=jnp.float32)
                 + lax.dot_general(up_grad, up_mat, contract, preferred_element_type=jnp.float32)).astype(jnp.bfloat16)
    down_grad = lax.dot_general(hidden, cotangent, (((0,), (0,)), ((), ())), preferred_element_type=jnp.float32).astype(jnp.bfloat16)
    return slot_grad, down_grad


def reference(tokens, assign, route_mask, match_mask, gate_weight, up_weight, down_weight, slow_down, momentum, slot_cot):
    sections, replicas, tok_rows, model_width = tokens.shape
    capacity = slot_cot.shape[3]
    hidden_width = gate_weight.shape[3]
    flat_tokens = tokens.reshape(sections * replicas, tok_rows, model_width)
    flat_ids = assign.reshape(sections * replicas, tok_rows)

    def dispatch_one(packet):
        rows, expert_ids = packet
        selector = slot_table(expert_ids, sections, capacity)
        placed = lax.dot_general(selector, rows, (((0,), (0,)), ((), ())), preferred_element_type=jnp.float32)
        return placed.astype(jnp.bfloat16).reshape(sections, capacity, model_width)

    dispatched = lax.map(dispatch_one, (flat_tokens, flat_ids)).reshape(sections, replicas, sections, capacity, model_width)

    def expert_one(index):
        expert = index // replicas
        replica = index % replicas
        source = jnp.bitwise_xor(replica, route_mask[expert])
        rows = dispatched[:, source, expert].reshape(-1, model_width)
        cotangent = slot_cot[expert, source].reshape(-1, model_width)
        slot_grad, down_grad = expert_pass(rows, cotangent, gate_weight[expert, replica], up_weight[expert, replica], down_weight[expert, replica])
        return slot_grad.reshape(sections, capacity, model_width), down_grad

    slot_grads, down_grads = lax.map(expert_one, jnp.arange(sections * replicas, dtype=jnp.int32))
    slot_grads = slot_grads.reshape(sections, replicas, sections, capacity, model_width)
    down_grads = down_grads.reshape(sections, replicas, hidden_width, model_width)

    slow_float = slow_down.astype(jnp.float32)
    delta = (slow_float - (down_weight.astype(jnp.float32) - inner_rate * down_grads.astype(jnp.float32))).astype(jnp.bfloat16)
    delta_float = delta.astype(jnp.float32)
    partner_term = (0.5 * delta_float - pull_rate * slow_float).astype(jnp.bfloat16)
    replica_range = jnp.arange(replicas, dtype=jnp.int32)
    partner_index = jnp.bitwise_xor(replica_range[None, :], match_mask[:, None])
    section_range = jnp.arange(sections, dtype=jnp.int32)[:, None]
    partner_value = partner_term[section_range, partner_index]
    outer_grad = 0.5 * delta_float + pull_rate * slow_float + partner_value.astype(jnp.float32)
    momentum_new = moment_rate * momentum.astype(jnp.float32) + outer_grad
    new_slow = (slow_float - outer_rate * (outer_grad + moment_rate * momentum_new)).astype(jnp.bfloat16)

    def return_one(index):
        section_id = index // replicas
        replica = index % replicas
        expert_ids = assign[section_id, replica, :, 0]
        sources = jnp.bitwise_xor(replica, route_mask)
        returned = slot_grads[jnp.arange(sections, dtype=jnp.int32), sources, section_id]
        selector = slot_table(expert_ids, sections, capacity)
        return jnp.dot(selector, returned.reshape(-1, model_width), preferred_element_type=jnp.float32).astype(jnp.bfloat16)

    input_grad = lax.map(return_one, jnp.arange(sections * replicas, dtype=jnp.int32))
    input_grad = input_grad.reshape(sections, replicas, tok_rows, model_width)
    return input_grad, new_slow
```

```python
import jax
import jax.numpy as jnp
from jax import lax
from jax.sharding import PartitionSpec as P

inner_rate = 0.05
pull_rate = 0.25
moment_rate = 0.9
outer_rate = 0.7


def xor_move(values, mask_value):
    replicas = lax.axis_size("rep")

    def branch(mask):
        pairs = [(source, source ^ mask) for source in range(replicas)]
        return lambda *arrays: tuple(lax.ppermute(array, "rep", pairs) for array in arrays)

    return lax.switch(mask_value - 1, [branch(mask) for mask in range(1, replicas)], *values)


def slot_table(expert_ids, sections, capacity):
    expert_hot = (expert_ids[:, None] == jnp.arange(sections, dtype=jnp.int32)[None, :]).astype(
        jnp.int32
    )
    position = jnp.sum((jnp.cumsum(expert_hot, axis=0) - 1) * expert_hot, axis=1)
    slot_index = expert_ids * capacity + position
    return (
        slot_index[:, None] == jnp.arange(sections * capacity, dtype=jnp.int32)[None, :]
    ).astype(jnp.bfloat16)


def expert_pass(rows, cotangent, gate_mat, up_mat, down_mat):
    contract = (((1,), (1,)), ((), ()))
    gate_act = jnp.dot(rows, gate_mat, preferred_element_type=jnp.float32)
    up_act = jnp.dot(rows, up_mat, preferred_element_type=jnp.float32)
    sigmoid_gate = jax.nn.sigmoid(gate_act)
    hidden = (gate_act * sigmoid_gate * up_act).astype(jnp.bfloat16)
    hidden_grad = lax.dot_general(cotangent, down_mat, contract, preferred_element_type=jnp.float32)
    gate_grad = (
        hidden_grad * up_act * sigmoid_gate * (1.0 + gate_act * (1.0 - sigmoid_gate))
    ).astype(jnp.bfloat16)
    up_grad = (hidden_grad * gate_act * sigmoid_gate).astype(jnp.bfloat16)
    slot_grad = (
        lax.dot_general(gate_grad, gate_mat, contract, preferred_element_type=jnp.float32)
        + lax.dot_general(up_grad, up_mat, contract, preferred_element_type=jnp.float32)
    ).astype(jnp.bfloat16)
    down_grad = lax.dot_general(
        hidden, cotangent, (((0,), (0,)), ((), ())), preferred_element_type=jnp.float32
    ).astype(jnp.bfloat16)
    return (slot_grad, down_grad)


def on_device(
    tokens,
    assign,
    route_mask,
    match_mask,
    gate_weight,
    up_weight,
    down_weight,
    slow_down,
    momentum,
    slot_cot,
):
    sections = lax.axis_size("section")
    section_here = lax.axis_index("section")
    token_rows = tokens[0, 0]
    expert_ids = assign[0, 0, :, 0]
    capacity = slot_cot.shape[3]
    model_width = token_rows.shape[1]
    down_mat = down_weight[0, 0]
    cotangent = slot_cot[0, 0]
    own_mask = route_mask[section_here]
    selector = slot_table(expert_ids, sections, capacity)
    placed = lax.dot_general(
        selector, token_rows, (((0,), (0,)), ((), ())), preferred_element_type=jnp.float32
    )
    dispatched = placed.astype(jnp.bfloat16).reshape(sections, capacity, model_width)
    arrived = lax.all_to_all(dispatched, "section", split_axis=0, concat_axis=0, tiled=True)
    both_here, down_here = xor_move(
        (jnp.concatenate([gate_weight[0, 0], up_weight[0, 0]], axis=0), down_mat), own_mask
    )
    gate_here, up_here = both_here[:model_width], both_here[model_width:]
    slot_grad, down_grad = expert_pass(
        arrived.reshape(-1, model_width),
        cotangent.reshape(-1, model_width),
        gate_here,
        up_here,
        down_here,
    )
    returned = lax.all_to_all(
        slot_grad.reshape(sections, capacity, model_width),
        "section",
        split_axis=0,
        concat_axis=0,
        tiled=True,
    )
    (down_grad,) = xor_move((down_grad,), own_mask)
    slow_mat = slow_down[0, 0]
    slow_float = slow_mat.astype(jnp.float32)
    delta = (
        slow_float - (down_mat.astype(jnp.float32) - inner_rate * down_grad.astype(jnp.float32))
    ).astype(jnp.bfloat16)
    delta_float = delta.astype(jnp.float32)
    partner_term = (0.5 * delta_float - pull_rate * slow_float).astype(jnp.bfloat16)
    (partner_value,) = xor_move((partner_term,), match_mask[section_here])
    outer_grad = 0.5 * delta_float + pull_rate * slow_float + partner_value.astype(jnp.float32)
    momentum_new = moment_rate * momentum[0, 0].astype(jnp.float32) + outer_grad
    new_slow = (slow_float - outer_rate * (outer_grad + moment_rate * momentum_new)).astype(
        jnp.bfloat16
    )
    input_grad = jnp.dot(
        selector, returned.reshape(-1, model_width), preferred_element_type=jnp.float32
    ).astype(jnp.bfloat16)
    return (input_grad[None, None], new_slow[None, None])


def solution(mesh):
    in_specs = (
        P("section", "rep", None, None),
        P("section", "rep", None, None),
        P(),
        P(),
        P("section", "rep", None, None),
        P("section", "rep", None, None),
        P("section", "rep", None, None),
        P("section", "rep", None, None),
        P("section", "rep", None, None),
        P("section", "rep", None, None, None),
    )
    out_specs = (P("section", "rep", None, None), P("section", "rep", None, None))
    return jax.shard_map(
        on_device, mesh=mesh, in_specs=in_specs, out_specs=out_specs, check_vma=False
    )
```
